1024 devices in a mesh: ri: 8 (over x, core), row: 8 (over y), col: 16 (over z).
Axes of the slice: x: 4, y: 8, z: 16, core: 2. Of those that a mesh axis runs over, the one named last changes fastest.
Arguments:
- three_centre: bfloat16 [64, 1024, 8192], P('ri', 'row', 'col'), may hold values from -0.5 to 0.5
- density_band: bfloat16 [8192, 5, 128], P('col'), may hold values from -0.25 to 0.25
- band_mask: int32 [64, 5], P('col'), may hold values 0 or 1
Outputs:
- exchange: float32 [1024, 1024], P('col', 'row')
The draws below stay inside these ranges and needn't reach their ends.
All inputs are finite; a program needn't handle non-finite values. No bound on the sum of `band_mask` on one device may be relied on, other than what follows from the above.
Results may differ from the reference program's by a relative error of at most 0.0029.
Values may be sent and summed in bfloat16 or wider, within the bound.
A program may use at most 32 MiB of HBM per device.

```python
import jax
import jax.numpy as jnp
from jax import lax

RI_DEV = 8
COL_ORB = 128
BLK_DEV = 4
BAND = 5
RI_FUNCS = 64
ROWS = 1024
COL_BLOCKS = 64
COLS = 8192
N_RI = 8
N_COL = 16


def plant(values, stream_key, low, high):
    dims = values.shape
    spot = [jax.random.randint(jax.random.fold_in(stream_key, axis), (), 0, dims[axis]) for axis in range(len(dims))]
    values = values.at[tuple(spot)].set(low)
    longest = dims.index(max(dims))
    spot[longest] = (spot[longest] + 1) % dims[longest]
    return values.at[tuple(spot)].set(high)


def block_levels(rng, dims, shards, smallest, high):
    def one(position, parts):
        steps = jax.random.uniform(jax.random.fold_in(jax.random.fold_in(rng, 6), position), (parts,), jnp.float32, smallest / len(shards), high / len(shards))
        return jnp.repeat(jnp.exp(steps), dims[position] // parts).reshape((-1,) + (1,) * (len(dims) - position - 1))

    factor_of = one(*shards[0])
    for cut in shards[1:]:
        factor_of = factor_of * one(*cut)
    return factor_of


def normal_values(rng, extent, deviation, reach, pieces=(), dtype=jnp.bfloat16):
    factor_of = block_levels(rng, extent, pieces, -0.22, 0.18) if pieces else 1.0
    drawn = jax.random.normal(rng, extent, jnp.float32) * deviation * factor_of
    return jnp.minimum(jnp.maximum(drawn, -reach), reach).astype(dtype)


def setup_inputs(seed: int = 0) -> dict:
    streams_of = jax.random.split(jax.random.key(seed), 4)
    three_centre = normal_values(streams_of[0], (RI_FUNCS, ROWS, COLS), ((RI_DEV * N_RI * COL_ORB * BLK_DEV * N_COL) ** -0.25), 0.5, ((0, 8), (1, 8), (2, 16)))
    density_band = normal_values(streams_of[1], (COLS, BAND, COL_ORB), (BAND * COL_ORB) ** -0.5, 0.25, ((0, 16),))
    band_mask = plant((jax.random.randint(streams_of[2], (COL_BLOCKS, BAND), 0, 4) < 3).astype(jnp.int32), jax.random.fold_in(streams_of[2], 1), 0, 1)
    return dict(three_centre=three_centre, density_band=density_band, band_mask=band_mask)


def reference(three_centre, density_band, band_mask):
    col_orb = density_band.shape[2]
    band_count = density_band.shape[1]
    centre = band_count // 2
    blocks = band_mask.shape[0]
    rows = three_centre.shape[1]
    weights = jnp.repeat(band_mask.astype(jnp.float32), col_orb, axis=0)[:, :, None]
    density = (density_band.astype(jnp.float32) * weights).astype(jnp.bfloat16)
    density_blocks = density.astype(jnp.float32).reshape(blocks, col_orb, band_count, col_orb)

    def one_function(total, tensor_row):
        tensor_full = tensor_row.astype(jnp.float32)
        tensor_blocks = tensor_full.reshape(rows, blocks, col_orb)
        mixed = jnp.zeros((rows, blocks, col_orb), jnp.float32)
        for column in range(band_count):
            part = jnp.einsum("mbl,bls->mbs", tensor_blocks, density_blocks[:, :, column, :])
            mixed = mixed + jnp.roll(part, column - centre, axis=1)
        mixed_low = lax.optimization_barrier(mixed.reshape(rows, blocks * col_orb).astype(jnp.bfloat16))
        mixed_back = mixed_low.astype(jnp.float32)
        return total + jnp.dot(tensor_full, mixed_back.T, preferred_element_type=jnp.float32), None

    start = jnp.zeros((rows, rows), jnp.float32)
    result, unused = lax.scan(one_function, start, three_centre)
    return result
```

```python
import jax
import jax.numpy as jnp
from jax import lax
from jax.experimental import pallas as pl
from jax.experimental.pallas import tpu as pltpu
from jax.sharding import PartitionSpec as P

CORES = 2
BF16 = jnp.bfloat16
F32 = jnp.float32


def arrival_order(length):
    order = [0]
    for step in range(1, length // 2 + 1):
        for offset in (step, (length - step) % length):
            if offset not in order:
                order.append(offset)
    return order


def make_kernel(nx, ny, nz, col_orb, blocks, band):
    centre = band // 2
    rim = centre * col_orb
    length = blocks * col_orb
    half = ny // CORES

    def kernel(
        tensor, density, mask, out,
        ext, dens, dens_low, dens_high, big, mixed,
        x_own, x_send, x_recv, z_send, z_recv, z_sum, y_send, y_recv, gathered,
        own_sem, a_send, a_recv, c_send, c_recv, hl_send, hl_recv, hr_send, hr_recv,
        d_sem, dl_send, dl_recv, dh_send, dh_recv,
        xs_sem, xr_sem, zs_sem, zr_sem, ys_sem, yr_sem, bs_sem, br_sem,
    ):
        ri = lax.axis_index("ri")
        y = lax.axis_index("row")
        z = lax.axis_index("col")
        x = ri // CORES
        core = lax.rem(ri, CORES)
        per_block = tensor.shape[1]
        owner = y // half

        def place(to_x=x, to_core=core, to_y=y, to_z=z):
            return {"ri": to_x * CORES + to_core, "row": to_y, "col": to_z}

        def send(source, target, send_sem, recv_sem, device):
            return pltpu.make_async_remote_copy(
                src_ref=source, dst_ref=target, send_sem=send_sem, recv_sem=recv_sem,
                device_id=device, device_id_type=pl.DeviceIdType.MESH,
            )

        z_up = lax.rem(z + 1, nz)
        z_down = lax.rem(z + nz - 1, nz)

        barrier = pltpu.get_barrier_semaphore()
        partners = [place(to_y=lax.rem(y + k, ny)) for k in range(1, ny)]
        partners += [place(to_z=lax.rem(z + k, nz)) for k in range(1, nz)]
        partners += [place(to_core=1 - core, to_z=z_up), place(to_core=1 - core, to_z=z_down)]
        partners += [place(to_core=1 - core)]
        for k in range(1, nx):
            for flip in (core, 1 - core):
                partners.append(place(to_x=lax.rem(x + k, nx), to_core=flip))
        for partner in partners:
            pl.semaphore_signal(barrier, inc=1, device_id=partner, device_id_type=pl.DeviceIdType.MESH)

        load = pltpu.make_async_copy(density, dens, d_sem)
        load.start()
        mine = pl.ds(y * per_block, per_block)
        middle = pl.ds(rim, length)
        own = pltpu.make_async_copy(tensor.at[y], ext.at[core, mine, :, :, middle], own_sem)
        own.start()
        big[...] = jnp.zeros_like(big)
        load.wait()
        for b in range(blocks):
            for c in range(band):
                weight = mask[b, c].astype(F32)
                rows = slice(b * col_orb, (b + 1) * col_orb)
                dens[c, rows, :] = (dens[c, rows, :].astype(F32) * weight).astype(BF16)
        pl.semaphore_wait(barrier, len(partners))

        started = []
        order = arrival_order(ny)
        for k in order[1:]:
            to = lax.rem(y + k, ny)
            copy = send(tensor.at[to], ext.at[core, mine, :, :, middle], a_send.at[k - 1], a_recv.at[k - 1], place(to_y=to))
            copy.start()
            started.append(copy)
        d_up = send(dens.at[pl.ds(centre + 1, centre), pl.ds(length - rim, rim)], dens_low, dl_send, dl_recv, place(to_z=z_up))
        d_down = send(dens.at[pl.ds(0, centre), pl.ds(0, rim)], dens_high, dh_send, dh_recv, place(to_z=z_down))
        d_up.start()
        d_down.start()

        def part(e, t):
            return slice((e % 2 + 2 * ((e - 2 * (t // 2)) // 2)) * col_orb, (e % 2 + 2 * ((e - 2 * (t // 2)) // 2) + 1) * col_orb), slice((t % 2) * col_orb, (t % 2 + 1) * col_orb)

        for t in range(blocks):
            for e in range(max(t, centre), min(t + band, centre + blocks)):
                rows, cols = part(e, t)
                local = e - centre
                big[t // 2, rows, cols] = dens[band - 1 - (e - t), local * col_orb : (local + 1) * col_orb, :]

        forwards = []
        for k in order:
            block = lax.rem(y + ny - k, ny)
            rows = pl.ds(block * per_block, per_block)
            if k == 0:
                own.wait()
            else:
                send(tensor.at[0], ext.at[core, rows, :, :, middle], a_send.at[k - 1], a_recv.at[k - 1], place()).wait_recv()
            whole = ext.at[core, rows, :, :, middle]
            to_half = block // half
            slot = lax.rem(block, half)
            over = send(whole, whole, c_send.at[k], c_recv.at[block], place(to_core=1 - core))
            left = send(ext.at[core, rows, :, :, pl.ds(rim, rim)], ext.at[core, rows, :, :, pl.ds(rim + length, rim)],
                        hr_send.at[k], hr_recv.at[core, slot], place(to_core=to_half, to_z=z_down))
            right = send(ext.at[core, rows, :, :, pl.ds(length, rim)], ext.at[core, rows, :, :, pl.ds(0, rim)],
                         hl_send.at[k], hl_recv.at[core, slot], place(to_core=to_half, to_z=z_up))
            for copy in (over, left, right):
                copy.start()
                forwards.append(copy)

        d_up.wait()
        d_down.wait()
        for t in range(blocks):
            for e in range(t, t + band):
                rows, cols = part(e, t)
                c = band - 1 - (e - t)
                if e < centre:
                    big[t // 2, rows, cols] = dens_low[c - centre - 1, e * col_orb : (e + 1) * col_orb, :]
                elif e >= centre + blocks:
                    at = e - centre - blocks
                    big[t // 2, rows, cols] = dens_high[c, at * col_orb : (at + 1) * col_orb, :]

        for slot in range(half):
            rows = pl.ds((core * half + slot) * per_block, per_block)
            for source in range(CORES):
                send(ext.at[0, rows, :, :, pl.ds(rim, rim)], ext.at[source, rows, :, :, pl.ds(rim + length, rim)],
                     hr_send.at[0], hr_recv.at[source, slot], place()).wait_recv()
                send(ext.at[0, rows, :, :, pl.ds(rim, rim)], ext.at[source, rows, :, :, pl.ds(0, rim)],
                     hl_send.at[0], hl_recv.at[source, slot], place()).wait_recv()
        for block in range(ny):
            rows = pl.ds(block * per_block, per_block)
            there = ext.at[1 - core, rows, :, :, middle]
            send(there, there, c_send.at[0], c_recv.at[block], place()).wait_recv()

        half_rows = half * per_block
        depth = big.shape[1]
        width = big.shape[2]
        m_rows = mixed.shape[0]
        for source in range(CORES):
            for u in range(big.shape[0]):
                rows = ext[source, pl.ds(core * half_rows, half_rows), :, :, u * width : u * width + depth].reshape(m_rows, depth)
                value = jnp.dot(rows, big[u], preferred_element_type=F32)
                mixed[:, source * length + u * width : source * length + (u + 1) * width] = value.astype(BF16)

        def terms(to):
            total = None
            for source in range(CORES):
                rows = ext[source, :, pl.ds(to, 1), :, rim : rim + length].reshape(-1, length)
                value = lax.dot_general(rows, mixed[:, source * length : (source + 1) * length],
                                        (((1,), (1,)), ((), ())), preferred_element_type=F32)
                total = value if total is None else total + value
            return total

        x_copies = []
        for k in range(1, nx):
            to = lax.rem(x + k, nx)
            x_send[k - 1] = terms(to).astype(BF16).reshape(x_send.shape[1:])
            copy = send(x_send.at[k - 1], x_recv.at[k - 1], xs_sem.at[k - 1], xr_sem.at[k - 1], place(to_x=to))
            copy.start()
            x_copies.append(copy)
        x_own[...] = terms(x).reshape(x_own.shape)
        for k in range(1, nx):
            x_copies[k - 1].wait_recv()
            x_own[...] += x_recv[k - 1].astype(F32)
        z_send[...] = x_own[...].astype(BF16)
        z_copies = []
        for k in range(1, nz):
            to = lax.rem(z + k, nz)
            copy = send(z_send.at[to], z_recv.at[k - 1], zs_sem.at[k - 1], zr_sem.at[k - 1], place(to_z=to))
            copy.start()
            z_copies.append(copy)
        z_sum[...] = x_own[z]
        for k in range(1, nz):
            z_copies[k - 1].wait_recv()
            z_sum[...] += z_recv[k - 1].astype(F32)
        for h in range(half):
            y_send[h] = z_sum[:, h * 128 : (h + 1) * 128]
        for h in range(half):
            to = core * half + h
            offset = lax.rem(to + ny - y, ny)

            @pl.when(to != y)
            def _(h=h, to=to, offset=offset):
                send(y_send.at[h], y_recv.at[offset - 1], ys_sem.at[h], yr_sem.at[offset - 1], place(to_y=to)).start()

        @pl.when(owner == core)
        def _():
            total = y_send[lax.rem(y, half)]
            for k in range(1, ny):
                send(y_send.at[0], y_recv.at[k - 1], ys_sem.at[0], yr_sem.at[k - 1], place()).wait_recv()
            for k in range(1, ny):
                total += y_recv[k - 1]
            gathered[x] = total
            for k in range(1, 2 * nx):
                device = {"ri": lax.rem(ri + k, CORES * nx), "row": y, "col": z}
                send(gathered.at[x], gathered.at[x], bs_sem.at[k - 1], br_sem.at[x], device).start()

        for k in range(nx):
            @pl.when((owner != core) | (k != x))
            def _(k=k):
                send(gathered.at[k], gathered.at[k], bs_sem.at[0], br_sem.at[k], place()).wait_recv()

        out[...] = gathered[...].reshape(out.shape)

        for copy in started:
            copy.wait_send()
        for copy in forwards:
            copy.wait_send()
        for copy in x_copies:
            copy.wait_send()
        for copy in z_copies:
            copy.wait_send()
        for h in range(half):
            @pl.when(core * half + h != y)
            def _(h=h):
                send(y_send.at[h], y_recv.at[0], ys_sem.at[h], yr_sem.at[0], place()).wait_send()

        @pl.when(owner == core)
        def _():
            for k in range(1, 2 * nx):
                send(gathered.at[x], gathered.at[x], bs_sem.at[k - 1], br_sem.at[x], place()).wait_send()

    return kernel


def solution(mesh):
    nx = mesh.shape["ri"] // CORES
    ny = mesh.shape["row"]
    nz = mesh.shape["col"]

    def per_device(three_centre, density_band, band_mask):
        funcs, block_rows, length = three_centre.shape
        blocks, band = band_mask.shape
        col_orb = density_band.shape[2]
        rows = block_rows * ny
        run = rows // (nz * nx)
        per_block = nz // ny
        centre = band // 2
        rim = centre * col_orb
        m_rows = rows // CORES
        half = ny // CORES
        tensor = three_centre.reshape(funcs, per_block, nx, run, length)
        density = jnp.transpose(density_band, (1, 0, 2))
        dma = pltpu.SemaphoreType.DMA
        return pl.pallas_call(
            make_kernel(nx, ny, nz, col_orb, blocks, band),
            out_shape=jax.ShapeDtypeStruct((rows // nz, block_rows), F32),
            in_specs=[
                pl.BlockSpec(memory_space=pl.ANY),
                pl.BlockSpec(memory_space=pl.ANY),
                pl.BlockSpec(memory_space=pltpu.SMEM),
            ],
            out_specs=pl.BlockSpec(memory_space=pltpu.VMEM),
            scratch_shapes=[
                pltpu.VMEM((CORES, nz, nx, run, length + 2 * rim), BF16),
                pltpu.VMEM(density.shape, BF16),
                pltpu.VMEM((centre, rim, col_orb), BF16),
                pltpu.VMEM((centre, rim, col_orb), BF16),
                pltpu.VMEM((blocks // 2, (band + 1) * col_orb, 2 * col_orb), BF16),
                pltpu.VMEM((m_rows, CORES * length), BF16),
                pltpu.VMEM((nz, run, m_rows), F32),
                pltpu.VMEM((nx - 1, nz, run, m_rows), BF16),
                pltpu.VMEM((nx - 1, nz, run, m_rows), BF16),
                pltpu.VMEM((nz, run, m_rows), BF16),
                pltpu.VMEM((nz - 1, run, m_rows), BF16),
                pltpu.VMEM((run, m_rows), F32),
                pltpu.VMEM((half, run, block_rows), F32),
                pltpu.VMEM((ny - 1, run, block_rows), F32),
                pltpu.VMEM((nx, run, block_rows), F32),
                dma, dma((ny - 1,)), dma((ny - 1,)), dma((ny,)), dma((ny,)),
                dma((ny,)), dma((CORES, half)), dma((ny,)), dma((CORES, half)),
                dma, dma, dma, dma, dma,
                dma((nx - 1,)), dma((nx - 1,)), dma((nz - 1,)), dma((nz - 1,)),
                dma((half,)), dma((ny - 1,)), dma((2 * nx - 1,)), dma((nx,)),
            ],
            compiler_params=pltpu.CompilerParams(
                collective_id=0, has_side_effects=True, vmem_limit_bytes=48 * 1024 * 1024
            ),
        )(tensor, density, band_mask)

    placed = (P("ri", "row", "col"), P("col", None, None), P("col", None))
    return jax.shard_map(
        per_device, mesh=mesh, in_specs=placed, out_specs=P("col", "row"), check_vma=False
    )
```

```python
import jax
import jax.numpy as jnp
from jax import lax
from jax.experimental import pallas as pl
from jax.experimental.pallas import tpu as pltpu
from jax.sharding import PartitionSpec as P

CORES = 2
BF16 = jnp.bfloat16
F32 = jnp.float32
MESH = pl.DeviceIdType.MESH


def remote(source, target, send_sem, recv_sem, device):
    return pltpu.make_async_remote_copy(
        src_ref=source, dst_ref=target, send_sem=send_sem, recv_sem=recv_sem,
        device_id=device, device_id_type=MESH,
    )


def make_kernel(nx, ny, nz, col_orb, blocks, band):
    centre = band // 2
    rim = centre * col_orb
    length = blocks * col_orb
    half = ny // CORES
    order = [0]
    for step in range(1, half):
        order += [step, ny - step]
    order.append(half)
    phases = [[0]] + [[2 * p - 1, 2 * p] for p in range(1, half)] + [[ny - 1]]

    def column_slot(offset):
        return (0, offset) if offset < half else (1, ny - 1 - offset)

    slot_at = {column_slot(offset): at for at, offset in enumerate(order)}

    def reach(p):
        rows = ny if p >= half else max(1 + 2 * p, 0)
        return rows, (min(max(p + 1, 0), half), max(p, 0))

    early = reach(half - 2)[0]

    def parts(side):
        found = []
        rows, slots = 0, 0
        for p in (half - 2, half - 1, half):
            now, upto = reach(p)
            upto = upto[side]
            found.append(((max(rows, early), now), (0, 0), (rows, now, 0, slots)))
            found.append(((0, 0), (slots, upto), (0, now, slots, upto)))
            rows, slots = now, upto
        return found

    def used(region):
        return region[1] > region[0] and region[3] > region[2]

    rounds = []
    while 2 ** len(rounds) < nz // 2:
        rounds.append(2 ** len(rounds))

    def kernel(
        tensor, density, band_mask, out,
        mask, ext, dens, dens_low, dens_high, big, mixed,
        x_own, x_send, x_recv, z_send, z_recv, y_send, y_recv, gathered,
        mask_sem, own_sem, a_send, a_recv, c_send, c_recv, h_send, h_recv, d_sem, d_send, d_recv,
        xs_sem, xr_sem, zs_sem, zr_sem, ys_sem, yr_sem, bs_sem, br_sem, far,
    ):
        state = []

        def phase(name):
            pass

        ri = lax.axis_index("ri")
        y = lax.axis_index("row")
        z = lax.axis_index("col")
        x = ri // CORES
        core = lax.rem(ri, CORES)
        per_block = tensor.shape[1]

        def place(to_x=x, to_core=core, to_y=y, to_z=z):
            return {"ri": to_x * CORES + to_core, "row": to_y, "col": to_z}

        z_up = lax.rem(z + 1, nz)
        z_down = lax.rem(z + nz - 1, nz)

        phase("p0_prep")
        barrier = pltpu.get_barrier_semaphore()
        partners = [place(to_y=lax.rem(y + k, ny)) for k in range(1, ny)]
        partners += [place(to_core=1 - core)]
        for k in range(1, nx):
            partners += [place(lax.rem(x + k, nx), flip) for flip in (core, 1 - core)]
        partners += [place(to_core=flip, to_z=to) for flip in (core, 1 - core) for to in (z_up, z_down)]
        for partner in partners:
            pl.semaphore_signal(barrier, inc=1, device_id=partner, device_id_type=MESH)

        load = pltpu.make_async_copy(density, dens, d_sem)
        load.start()
        masks = pltpu.make_async_copy(band_mask, mask, mask_sem)
        masks.start()
        middle = pl.ds(rim, length)
        own = pltpu.make_async_copy(tensor.at[y], ext.at[core, 0, :, :, :, middle], own_sem)
        own.start()
        big[...] = jnp.zeros_like(big)
        load.wait()
        masks.wait()
        for b in range(blocks):
            for c in range(band):
                weight = mask[b, c].astype(F32)
                rows = slice(b * col_orb, (b + 1) * col_orb)
                dens[c, rows, :] = (dens[c, rows, :].astype(F32) * weight).astype(BF16)
        phase("p1_barrier")
        pl.semaphore_wait(barrier, len(partners))
        phase("p2_start")

        def far_signal(r):
            for side, to in ((0, lax.rem(z + nz - rounds[r], nz)), (1, lax.rem(z + rounds[r], nz))):
                pl.semaphore_signal(far.at[r, side], inc=1, device_id=place(to_z=to), device_id_type=MESH)

        def far_wait(r):
            for side in range(2):
                pl.semaphore_wait(far.at[r, side], 1)

        started = [None]
        for at in range(1, ny):
            to = lax.rem(y + ny - order[at], ny)
            started.append(remote(tensor.at[to], ext.at[core, at, :, :, :, middle], a_send, a_recv.at[at - 1], place(to_y=to)))

        def begin(p):
            if 0 < p <= half:
                for at in phases[p]:
                    started[at].start()

        begin(1)
        begin(2)
        d_up = remote(dens.at[pl.ds(centre + 1, centre), pl.ds(length - rim, rim)], dens_low, d_send, d_recv, place(to_z=z_up))
        d_down = remote(dens.at[pl.ds(0, centre), pl.ds(0, rim)], dens_high, d_send, d_recv, place(to_z=z_down))
        d_up.start()
        d_down.start()
        if rounds:
            far_signal(0)

        def tile(e, t):
            row, col = e - 2 * (t // 2), t % 2
            return slice(row * col_orb, (row + 1) * col_orb), slice(col * col_orb, (col + 1) * col_orb)

        for t in range(blocks):
            for e in range(max(t, centre), min(t + band, centre + blocks)):
                rows, cols = tile(e, t)
                local = e - centre
                big[t // 2, rows, cols] = dens[band - 1 - (e - t), local * col_orb : (local + 1) * col_orb, :]

        def halo_copies(at, source):
            side, slot = column_slot(order[at])
            left = remote(ext.at[source, at, :, :, :, pl.ds(rim, rim)], ext.at[source, at, :, :, :, pl.ds(rim + length, rim)],
                          h_send, h_recv.at[slot], place(to_core=side, to_z=z_down))
            right = remote(ext.at[source, at, :, :, :, pl.ds(length, rim)], ext.at[source, at, :, :, :, pl.ds(0, rim)],
                           h_send, h_recv.at[slot], place(to_core=side, to_z=z_up))
            return left, right

        def over_copy(at, source):
            whole = ext.at[source, at, :, :, :, middle]
            return remote(whole, whole, c_send, c_recv.at[at], place(to_core=1 - core))

        def forward(p):
            for at in phases[p]:
                phase(f"p3_arrive{at}")
                if at == 0:
                    own.wait()
                else:
                    started[at].wait_recv()
                for copy in (*halo_copies(at, core), over_copy(at, core)):
                    copy.start()

        def density_rims():
            both = dens.at[pl.ds(0, centre), pl.ds(0, 2 * rim)]
            remote(both, both, d_send, d_recv, place()).wait()
            for t in range(blocks):
                for e in range(t, t + band):
                    rows, cols = tile(e, t)
                    c = band - 1 - (e - t)
                    if e < centre:
                        big[t // 2, rows, cols] = dens_low[c - centre - 1, e * col_orb : (e + 1) * col_orb, :]
                    elif e >= centre + blocks:
                        to = e - centre - blocks
                        big[t // 2, rows, cols] = dens_high[c, to * col_orb : (to + 1) * col_orb, :]

        depth = big.shape[1]
        width = big.shape[2]

        def mix(side, slot):
            at = slot_at[side, slot]
            for source in range(CORES):
                for u in range(big.shape[0]):
                    rows = ext[source, at, :, :, :, u * width : u * width + depth].reshape(-1, depth)
                    value = jnp.dot(rows, big[u], preferred_element_type=F32)
                    at_row = source * length + u * width
                    mixed[at_row : at_row + width, slot * 128 : (slot + 1) * 128] = value.T.astype(BF16)

        def terms(region):
            n0, n1, m0, m1 = region
            total = None
            for source in range(CORES):
                rows = ext[source, n0:n1, :, :, :, rim : rim + length].reshape(-1, length)
                value = jnp.dot(rows, mixed[source * length : (source + 1) * length, m0 * 128 : m1 * 128], preferred_element_type=F32)
                total = value if total is None else total + value
            total = total.reshape(n1 - n0, per_block, nx, -1, (m1 - m0) * 128)
            kept = None
            for to in range(nx):
                value = total[:, :, to]
                x_send[to, n0:n1, :, :, m0 * 128 : m1 * 128] = value.astype(BF16)
                kept = value if kept is None else jnp.where(x == to, value, kept)
            x_own[n0:n1, :, :, m0 * 128 : m1 * 128] = kept

        def x_copy(k, part, region):
            n0, n1, m0, m1 = region
            at = (pl.ds(n0, n1 - n0), slice(None), slice(None), pl.ds(m0 * 128, (m1 - m0) * 128))
            to = lax.rem(x + k, nx)
            return remote(x_send.at[(to, *at)], x_recv.at[(k - 1, *at)], xs_sem, xr_sem.at[part],
                          place(to_x=to))

        def advance(*chosen):
            for side in range(CORES):
                @pl.when(core == side)
                def _(side=side):
                    for part in chosen:
                        arrived, mixing, region = parts(side)[part]
                        for slot in range(*mixing):
                            rims = ext.at[:, slot_at[side, slot], :, :, :, pl.ds(0, 2 * rim)]
                            remote(rims, rims, h_send, h_recv.at[slot], place()).wait_recv()
                        for at in range(*arrived):
                            over_copy(at, 1 - side).wait_recv()
                        for slot in range(*mixing):
                            mix(side, slot)
                        if not used(region):
                            continue
                        terms(region)
                        for k in range(1, nx):
                            x_copy(k, part, region).start()

        sent, waited = 1, 0
        for p in range(max(half - 1, 0)):
            forward(p)
            for at in phases[p]:
                over_copy(at, 1 - core).wait_recv()
            if p > 0:
                begin(p + 2)
            if 1 <= p < len(rounds):
                far_wait(p - 1)
                far_signal(p)
                sent, waited = p + 1, p
        density_rims()
        def z_copy(part, region, at, b):
            lanes = pl.ds(region[2] * 128, (region[3] - region[2]) * 128)
            to = lax.rem(y + order[at], ny) * per_block + b
            k = lax.rem(to + nz - z, nz)
            slot = lax.rem(k + nz - 1, nz)
            return k, remote(z_send.at[to, :, lanes], z_recv.at[slot, :, lanes], zs_sem, zr_sem,
                             place(to_z=to))

        def settle(*chosen):
            for side in range(CORES):
                @pl.when(core == side)
                def _(side=side):
                    for part in chosen:
                        region = parts(side)[part][2]
                        if not used(region):
                            continue
                        n0, n1, m0, m1 = region
                        lanes = pl.ds(m0 * 128, (m1 - m0) * 128)
                        landed = x_recv.at[:, pl.ds(n0, n1 - n0), :, :, lanes]
                        remote(landed, landed, xs_sem, xr_sem.at[part], place()).wait_recv()
                        for at in range(n0, n1):
                            total = x_own[at, :, :, lanes]
                            for k in range(1, nx):
                                total += x_recv[k - 1, at, :, :, lanes].astype(F32)
                            block = lax.rem(y + order[at], ny)
                            x_own[at, :, :, lanes] = total
                            z_send[pl.ds(block * per_block, per_block), :, lanes] = total.astype(BF16)

                            @pl.when(block == z // per_block)
                            def _(at=at, lanes=lanes):
                                y_send[:, lanes] = x_own[at, lax.rem(z, per_block), :, lanes]
                        for at in range(n0, n1):
                            for b in range(per_block):
                                k, copy = z_copy(part, region, at, b)

                                @pl.when(k != 0)
                                def _(copy=copy):
                                    copy.start()

        phase("p4_a")
        advance(0, 1)
        forward(half - 1)
        phase("p4_b1")
        advance(2)
        for r in range(waited, len(rounds)):
            if r >= sent:
                far_signal(r)
            far_wait(r)
        phase("p5_za")
        settle(0, 1)
        phase("p4_b2")
        advance(3)
        forward(half)
        phase("p4_c1")
        advance(4)
        phase("p4_c2")
        advance(5)
        phase("p5_zb")
        settle(2, 3)
        phase("p5_zc")
        settle(4, 5)
        phase("p7_zwait")
        landed = z_recv.at[pl.ds(0, nz - 1)]
        remote(landed, landed, zs_sem, zr_sem, place()).wait_recv()
        total = y_send[...]
        for slot in range(nz - 1):
            total += z_recv[slot].astype(F32)
        for slot in range(half):
            y_recv[half + slot] = total[:, slot * 128 : (slot + 1) * 128]
        phase("p8_ywait")

        def y_copy(slot):
            to = lax.rem(y + core * (ny - 1) + slot * (1 - 2 * core), ny)
            return remote(y_recv.at[half + slot], y_recv.at[slot], ys_sem, yr_sem, place(to_y=to))

        def y_all(side):
            whole = y_recv.at[pl.ds(0, half - 1 + side)]
            return remote(whole, whole, ys_sem, yr_sem, place())

        for slot in range(1, half):
            y_copy(slot).start()
        for side in range(CORES):
            @pl.when(core == side)
            def _(side=side):
                if side == 1:
                    y_copy(0).start()
                if half - 1 + side > 0:
                    y_all(side).wait_recv()
                if side == 0:
                    y_recv[0] = y_recv[half]

        total = y_recv[0]
        for slot in range(1, half):
            total += y_recv[slot]
        gathered[ri] = total
        phase("p9_bwait")

        def b_copy(k, source):
            device = {"ri": lax.rem(ri + k, CORES * nx), "row": y, "col": z}
            return remote(gathered.at[source], gathered.at[source], bs_sem, br_sem, device)

        for k in range(1, CORES * nx):
            b_copy(k, ri).start()
        spread = gathered.at[pl.ds(0, CORES * nx - 1)]
        remote(spread, spread, bs_sem, br_sem, place()).wait_recv()
        run = gathered.shape[1]
        for k in range(nx):
            out[k * run : (k + 1) * run, :] = gathered[CORES * k] + gathered[CORES * k + 1]
        phase("pa_end")

        for view, sem in (
            (ext.at[core, pl.ds(1, ny - 1), :, :, :, middle], a_send),
            (ext.at[core, :, :, :, :, middle], c_send),
            (ext.at[core, :, :, :, :, pl.ds(0, 2 * rim)], h_send),
            (x_send.at[pl.ds(0, nx - 1)], xs_sem),
            (z_send.at[pl.ds(0, nz - 1)], zs_sem),
            (spread, bs_sem),
        ):
            remote(view, view, sem, sem, place()).wait_send()
        for side in range(CORES):
            @pl.when(core == side)
            def _(side=side):
                if half - 1 + side > 0:
                    y_all(side).wait_send()
        phase(None)

    return kernel, max(len(rounds), 1)


def solution(mesh):
    nx = mesh.shape["ri"] // CORES
    ny = mesh.shape["row"]
    nz = mesh.shape["col"]

    def per_device(three_centre, density_band, band_mask):
        funcs, block_rows, length = three_centre.shape
        blocks, band = band_mask.shape
        col_orb = density_band.shape[2]
        rows = block_rows * ny
        run = rows // (nz * nx)
        per_block = nz // ny
        centre = band // 2
        rim = centre * col_orb
        half = ny // CORES
        m_rows = half * block_rows
        tensor = three_centre.reshape(funcs, per_block, nx, run, length)
        density = jnp.transpose(density_band, (1, 0, 2))
        dma = pltpu.SemaphoreType.DMA
        kernel, rounds = make_kernel(nx, ny, nz, col_orb, blocks, band)
        return pl.pallas_call(
            kernel,
            out_shape=jax.ShapeDtypeStruct((rows // nz, block_rows), F32),
            in_specs=[
                pl.BlockSpec(memory_space=pltpu.HBM),
                pl.BlockSpec(memory_space=pltpu.HBM),
                pl.BlockSpec(memory_space=pltpu.HBM),
            ],
            out_specs=pl.BlockSpec(memory_space=pltpu.VMEM),
            scratch_shapes=[
                pltpu.SMEM((blocks, band), jnp.int32),
                pltpu.VMEM((CORES, ny, per_block, nx, run, length + 2 * rim), BF16),
                pltpu.VMEM(density.shape, BF16),
                pltpu.VMEM((centre, rim, col_orb), BF16),
                pltpu.VMEM((centre, rim, col_orb), BF16),
                pltpu.VMEM((blocks // 2, (band + 1) * col_orb, 2 * col_orb), BF16),
                pltpu.VMEM((CORES * length, m_rows), BF16),
                pltpu.VMEM((ny, per_block, run, m_rows), F32),
                pltpu.VMEM((nx, ny, per_block, run, m_rows), BF16),
                pltpu.VMEM((nx - 1, ny, per_block, run, m_rows), BF16),
                pltpu.VMEM((nz, run, m_rows), BF16),
                pltpu.VMEM((nz, run, m_rows), BF16),
                pltpu.VMEM((run, m_rows), F32),
                pltpu.VMEM((2 * half, run, block_rows), F32),
                pltpu.VMEM((CORES * nx, run, block_rows), F32),
                dma, dma, dma, dma((ny - 1,)), dma, dma((ny,)), dma, dma((half,)), dma, dma, dma,
                dma, dma((6,)), dma, dma, dma, dma, dma, dma,
                pltpu.SemaphoreType.REGULAR((rounds, 2)),
            ],
            compiler_params=pltpu.CompilerParams(
                collective_id=0, has_side_effects=True, vmem_limit_bytes=67043328
            ),
        )(tensor, density, band_mask)

    placed = (P("ri", "row", "col"), P("col", None, None), P("col", None))
    return jax.shard_map(
        per_device, mesh=mesh, in_specs=placed, out_specs=P("col", "row"), check_vma=False
    )
```

```python
import jax
import jax.numpy as jnp
from jax import lax
from jax.experimental import pallas as pl
from jax.experimental.pallas import tpu as pltpu
from jax.sharding import PartitionSpec as P

CORES = 2
BF16 = jnp.bfloat16
F32 = jnp.float32
MESH = pl.DeviceIdType.MESH


def remote(source, target, send_sem, recv_sem, device):
    return pltpu.make_async_remote_copy(
        src_ref=source, dst_ref=target, send_sem=send_sem, recv_sem=recv_sem,
        device_id=device, device_id_type=MESH,
    )


def make_kernel(nx, ny, nz, col_orb, blocks, band):
    centre = band // 2
    rim = centre * col_orb
    length = blocks * col_orb
    half = ny // CORES
    order = [0]
    for step in range(1, half):
        order += [step, ny - step]
    order.append(half)
    phases = [[0]] + [[2 * p - 1, 2 * p] for p in range(1, half)] + [[ny - 1]]

    def column_slot(offset):
        return (0, offset) if offset < half else (1, ny - 1 - offset)

    slot_at = {column_slot(offset): at for at, offset in enumerate(order)}

    def reach(p):
        rows = ny if p >= half else max(1 + 2 * p, 0)
        return rows, (min(max(p + 1, 0), half), max(p, 0))

    early = reach(half - 2)[0]

    def parts(side):
        found = []
        rows, slots = 0, 0
        for p in (half - 3, half - 2, half - 1, half):
            now, upto = reach(p)
            upto = upto[side]
            found.append(((max(rows, early), max(now, early)), (0, 0), (rows, now, 0, slots)))
            found.append(((0, 0), (slots, upto), (0, now, slots, upto)))
            rows, slots = now, upto
        return found

    def used(region):
        return region[1] > region[0] and region[3] > region[2]

    rounds = []
    while 2 ** len(rounds) < nz // 2:
        rounds.append(2 ** len(rounds))

    def kernel(
        tensor, density, band_mask, out,
        mask, ext, dens, dens_low, dens_high, big, mixed,
        x_own, x_send, x_recv, z_send, z_recv, y_send, y_recv, gathered,
        mask_sem, own_sem, a_send, a_recv, c_send, c_recv, h_send, h_recv, d_sem, d_send, d_recv,
        xs_sem, xr_sem, zs_sem, zr_sem, ys_sem, yr_sem, bs_sem, br_sem, far,
    ):
        state = []

        def phase(name):
            pass

        ri = lax.axis_index("ri")
        y = lax.axis_index("row")
        z = lax.axis_index("col")
        x = ri // CORES
        core = lax.rem(ri, CORES)
        per_block = tensor.shape[1]

        def place(to_x=x, to_core=core, to_y=y, to_z=z):
            return {"ri": to_x * CORES + to_core, "row": to_y, "col": to_z}

        z_up = lax.rem(z + 1, nz)
        z_down = lax.rem(z + nz - 1, nz)

        phase("p0_prep")
        barrier = pltpu.get_barrier_semaphore()
        partners = [place(to_y=lax.rem(y + k, ny)) for k in range(1, ny)]
        partners += [place(to_core=1 - core)]
        for k in range(1, nx):
            partners += [place(lax.rem(x + k, nx), flip) for flip in (core, 1 - core)]
        partners += [place(to_core=flip, to_z=to) for flip in (core, 1 - core) for to in (z_up, z_down)]
        for partner in partners:
            pl.semaphore_signal(barrier, inc=1, device_id=partner, device_id_type=MESH)

        load = pltpu.make_async_copy(density, dens, d_sem)
        load.start()
        masks = pltpu.make_async_copy(band_mask, mask, mask_sem)
        masks.start()
        middle = pl.ds(rim, length)
        own = pltpu.make_async_copy(tensor.at[y], ext.at[core, 0, :, :, :, middle], own_sem)
        own.start()
        big[...] = jnp.zeros_like(big)
        phase("p1_barrier")
        pl.semaphore_wait(barrier, len(partners))
        phase("p2_start")

        def far_signal(r):
            for side, to in ((0, lax.rem(z + nz - rounds[r], nz)), (1, lax.rem(z + rounds[r], nz))):
                pl.semaphore_signal(far.at[r, side], inc=1, device_id=place(to_z=to), device_id_type=MESH)

        def far_wait(r):
            for side in range(2):
                pl.semaphore_wait(far.at[r, side], 1)

        started = [None]
        for at in range(1, ny):
            to = lax.rem(y + ny - order[at], ny)
            started.append(remote(tensor.at[to], ext.at[core, at, :, :, :, middle], a_send, a_recv.at[at - 1], place(to_y=to)))

        def begin(p):
            if 0 < p <= half:
                for at in phases[p]:
                    started[at].start()

        begin(1)
        begin(2)
        load.wait()
        masks.wait()
        for b in range(blocks):
            for c in range(band):
                weight = mask[b, c].astype(F32)
                rows = slice(b * col_orb, (b + 1) * col_orb)
                dens[c, rows, :] = (dens[c, rows, :].astype(F32) * weight).astype(BF16)
        d_up = remote(dens.at[pl.ds(centre + 1, centre), pl.ds(length - rim, rim)], dens_low, d_send, d_recv, place(to_z=z_up))
        d_down = remote(dens.at[pl.ds(0, centre), pl.ds(0, rim)], dens_high, d_send, d_recv, place(to_z=z_down))
        d_up.start()
        d_down.start()
        if rounds:
            far_signal(0)

        def tile(e, t):
            row, col = e - 2 * (t // 2), t % 2
            return slice(row * col_orb, (row + 1) * col_orb), slice(col * col_orb, (col + 1) * col_orb)

        for t in range(blocks):
            for e in range(max(t, centre), min(t + band, centre + blocks)):
                rows, cols = tile(e, t)
                local = e - centre
                big[t // 2, rows, cols] = dens[band - 1 - (e - t), local * col_orb : (local + 1) * col_orb, :]

        def halo_copies(at, source):
            side, slot = column_slot(order[at])
            left = remote(ext.at[source, at, :, :, :, pl.ds(rim, rim)], ext.at[source, at, :, :, :, pl.ds(rim + length, rim)],
                          h_send, h_recv.at[slot], place(to_core=side, to_z=z_down))
            right = remote(ext.at[source, at, :, :, :, pl.ds(length, rim)], ext.at[source, at, :, :, :, pl.ds(0, rim)],
                           h_send, h_recv.at[slot], place(to_core=side, to_z=z_up))
            return left, right

        def over_copy(at, source):
            whole = ext.at[source, at, :, :, :, middle]
            return remote(whole, whole, c_send, c_recv.at[at], place(to_core=1 - core))

        def forward(p):
            for at in phases[p]:
                phase(f"p3_arrive{at}")
                if at == 0:
                    own.wait()
                else:
                    started[at].wait_recv()
                for copy in (*halo_copies(at, core), over_copy(at, core)):
                    copy.start()

        def density_rims():
            both = dens.at[pl.ds(0, centre), pl.ds(0, 2 * rim)]
            remote(both, both, d_send, d_recv, place()).wait()
            for t in range(blocks):
                for e in range(t, t + band):
                    rows, cols = tile(e, t)
                    c = band - 1 - (e - t)
                    if e < centre:
                        big[t // 2, rows, cols] = dens_low[c - centre - 1, e * col_orb : (e + 1) * col_orb, :]
                    elif e >= centre + blocks:
                        to = e - centre - blocks
                        big[t // 2, rows, cols] = dens_high[c, to * col_orb : (to + 1) * col_orb, :]

        depth = big.shape[1]
        width = big.shape[2]

        def mix(side, slot):
            at = slot_at[side, slot]
            for source in range(CORES):
                for u in range(big.shape[0]):
                    rows = ext[source, at, :, :, :, u * width : u * width + depth].reshape(-1, depth)
                    value = jnp.dot(rows, big[u], preferred_element_type=F32)
                    at_row = source * length + u * width
                    mixed[at_row : at_row + width, slot * 128 : (slot + 1) * 128] = value.T.astype(BF16)

        def terms(region):
            n0, n1, m0, m1 = region
            total = None
            for source in range(CORES):
                rows = ext[source, n0:n1, :, :, :, rim : rim + length].reshape(-1, length)
                value = jnp.dot(rows, mixed[source * length : (source + 1) * length, m0 * 128 : m1 * 128], preferred_element_type=F32)
                total = value if total is None else total + value
            total = total.reshape(n1 - n0, per_block, nx, -1, (m1 - m0) * 128)
            kept = None
            for to in range(nx):
                value = total[:, :, to]
                x_send[to, n0:n1, :, :, m0 * 128 : m1 * 128] = value.astype(BF16)
                kept = value if kept is None else jnp.where(x == to, value, kept)
            x_own[n0:n1, :, :, m0 * 128 : m1 * 128] = kept

        def x_copy(k, part, region):
            n0, n1, m0, m1 = region
            at = (pl.ds(n0, n1 - n0), slice(None), slice(None), pl.ds(m0 * 128, (m1 - m0) * 128))
            to = lax.rem(x + k, nx)
            return remote(x_send.at[(to, *at)], x_recv.at[(k - 1, *at)], xs_sem, xr_sem.at[part],
                          place(to_x=to))

        def advance(*chosen):
            for side in range(CORES):
                @pl.when(core == side)
                def _(side=side):
                    for part in chosen:
                        arrived, mixing, region = parts(side)[part]
                        for slot in range(*mixing):
                            rims = ext.at[:, slot_at[side, slot], :, :, :, pl.ds(0, 2 * rim)]
                            remote(rims, rims, h_send, h_recv.at[slot], place()).wait_recv()
                        for at in range(*arrived):
                            over_copy(at, 1 - side).wait_recv()
                        for slot in range(*mixing):
                            mix(side, slot)
                        if not used(region):
                            continue
                        terms(region)
                        for k in range(1, nx):
                            x_copy(k, part, region).start()

        def z_copy(part, region, at, b):
            lanes = pl.ds(region[2] * 128, (region[3] - region[2]) * 128)
            to = lax.rem(y + order[at], ny) * per_block + b
            k = lax.rem(to + nz - z, nz)
            slot = lax.rem(k + nz - 1, nz)
            return k, remote(z_send.at[to, :, lanes], z_recv.at[slot, :, lanes], zs_sem, zr_sem,
                             place(to_z=to))

        def settle(*chosen):
            for side in range(CORES):
                @pl.when(core == side)
                def _(side=side):
                    for part in chosen:
                        region = parts(side)[part][2]
                        if not used(region):
                            continue
                        n0, n1, m0, m1 = region
                        lanes = pl.ds(m0 * 128, (m1 - m0) * 128)
                        landed = x_recv.at[:, pl.ds(n0, n1 - n0), :, :, lanes]
                        remote(landed, landed, xs_sem, xr_sem.at[part], place()).wait_recv()
                        for at in range(n0, n1):
                            total = x_own[at, :, :, lanes]
                            for k in range(1, nx):
                                total += x_recv[k - 1, at, :, :, lanes].astype(F32)
                            block = lax.rem(y + order[at], ny)
                            x_own[at, :, :, lanes] = total
                            z_send[pl.ds(block * per_block, per_block), :, lanes] = total.astype(BF16)

                            @pl.when(block == z // per_block)
                            def _(at=at, lanes=lanes):
                                y_send[:, lanes] = x_own[at, lax.rem(z, per_block), :, lanes]
                        for at in range(n0, n1):
                            for b in range(per_block):
                                k, copy = z_copy(part, region, at, b)

                                @pl.when(k != 0)
                                def _(copy=copy):
                                    copy.start()

        sent, waited = 1, 0
        for p in range(max(half - 1, 0)):
            forward(p)
            if p == half - 2:
                density_rims()
                phase("p4_a0")
                advance(0, 1)
                phase("p4_over")
            for at in phases[p]:
                over_copy(at, 1 - core).wait_recv()
            if 0 < p < half - 2:
                begin(p + 2)
            if 1 <= p < len(rounds):
                far_wait(p - 1)
                far_signal(p)
                sent, waited = p + 1, p
        if half == 1:
            density_rims()
        phase("p4_a1")
        advance(2, 3)
        forward(half - 1)
        if half > 2:
            begin(half)
        phase("p4_b1")
        advance(4)
        for r in range(waited, len(rounds)):
            if r >= sent:
                far_signal(r)
            far_wait(r)
        phase("p5_za")
        settle(0, 1, 2, 3)
        phase("p4_b2")
        advance(5)
        forward(half)
        phase("p4_c1")
        advance(6)
        phase("p4_c2")
        advance(7)
        phase("p5_zb")
        settle(4, 5)
        phase("p5_zc")
        settle(6, 7)
        phase("p7_zwait")
        landed = z_recv.at[pl.ds(0, nz - 1)]
        remote(landed, landed, zs_sem, zr_sem, place()).wait_recv()
        total = y_send[...]
        for slot in range(nz - 1):
            total += z_recv[slot].astype(F32)
        for slot in range(half):
            y_recv[half + slot] = total[:, slot * 128 : (slot + 1) * 128]
        phase("p8_ywait")

        def y_copy(slot):
            to = lax.rem(y + core * (ny - 1) + slot * (1 - 2 * core), ny)
            return remote(y_recv.at[half + slot], y_recv.at[slot], ys_sem, yr_sem, place(to_y=to))

        def y_all(side):
            whole = y_recv.at[pl.ds(0, half - 1 + side)]
            return remote(whole, whole, ys_sem, yr_sem, place())

        for slot in range(1, half):
            y_copy(slot).start()
        for side in range(CORES):
            @pl.when(core == side)
            def _(side=side):
                if side == 1:
                    y_copy(0).start()
                if half - 1 + side > 0:
                    y_all(side).wait_recv()
                if side == 0:
                    y_recv[0] = y_recv[half]

        total = y_recv[0]
        for slot in range(1, half):
            total += y_recv[slot]
        gathered[ri] = total
        phase("p9_bwait")

        def b_copy(k, source):
            device = {"ri": lax.rem(ri + k, CORES * nx), "row": y, "col": z}
            return remote(gathered.at[source], gathered.at[source], bs_sem, br_sem, device)

        for k in range(1, CORES * nx):
            b_copy(k, ri).start()
        spread = gathered.at[pl.ds(0, CORES * nx - 1)]
        remote(spread, spread, bs_sem, br_sem, place()).wait_recv()
        run = gathered.shape[1]
        for k in range(nx):
            out[k * run : (k + 1) * run, :] = gathered[CORES * k] + gathered[CORES * k + 1]
        phase("pa_end")

        for view, sem in (
            (ext.at[core, pl.ds(1, ny - 1), :, :, :, middle], a_send),
            (ext.at[core, :, :, :, :, middle], c_send),
            (ext.at[core, :, :, :, :, pl.ds(0, 2 * rim)], h_send),
            (x_send.at[pl.ds(0, nx - 1)], xs_sem),
            (z_send.at[pl.ds(0, nz - 1)], zs_sem),
            (spread, bs_sem),
        ):
            remote(view, view, sem, sem, place()).wait_send()
        for side in range(CORES):
            @pl.when(core == side)
            def _(side=side):
                if half - 1 + side > 0:
                    y_all(side).wait_send()
        phase(None)

    return kernel, max(len(rounds), 1)


def solution(mesh):
    nx = mesh.shape["ri"] // CORES
    ny = mesh.shape["row"]
    nz = mesh.shape["col"]

    def per_device(three_centre, density_band, band_mask):
        funcs, block_rows, length = three_centre.shape
        blocks, band = band_mask.shape
        col_orb = density_band.shape[2]
        rows = block_rows * ny
        run = rows // (nz * nx)
        per_block = nz // ny
        centre = band // 2
        rim = centre * col_orb
        half = ny // CORES
        m_rows = half * block_rows
        tensor = three_centre.reshape(funcs, per_block, nx, run, length)
        density = jnp.transpose(density_band, (1, 0, 2))
        dma = pltpu.SemaphoreType.DMA
        kernel, rounds = make_kernel(nx, ny, nz, col_orb, blocks, band)
        return pl.pallas_call(
            kernel,
            out_shape=jax.ShapeDtypeStruct((rows // nz, block_rows), F32),
            in_specs=[
                pl.BlockSpec(memory_space=pltpu.HBM),
                pl.BlockSpec(memory_space=pltpu.HBM),
                pl.BlockSpec(memory_space=pltpu.HBM),
            ],
            out_specs=pl.BlockSpec(memory_space=pltpu.VMEM),
            scratch_shapes=[
                pltpu.SMEM((blocks, band), jnp.int32),
                pltpu.VMEM((CORES, ny, per_block, nx, run, length + 2 * rim), BF16),
                pltpu.VMEM(density.shape, BF16),
                pltpu.VMEM((centre, rim, col_orb), BF16),
                pltpu.VMEM((centre, rim, col_orb), BF16),
                pltpu.VMEM((blocks // 2, (band + 1) * col_orb, 2 * col_orb), BF16),
                pltpu.VMEM((CORES * length, m_rows), BF16),
                pltpu.VMEM((ny, per_block, run, m_rows), F32),
                pltpu.VMEM((nx, ny, per_block, run, m_rows), BF16),
                pltpu.VMEM((nx - 1, ny, per_block, run, m_rows), BF16),
                pltpu.VMEM((nz, run, m_rows), BF16),
                pltpu.VMEM((nz, run, m_rows), BF16),
                pltpu.VMEM((run, m_rows), F32),
                pltpu.VMEM((2 * half, run, block_rows), F32),
                pltpu.VMEM((CORES * nx, run, block_rows), F32),
                dma, dma, dma, dma((ny - 1,)), dma, dma((ny,)), dma, dma((half,)), dma, dma, dma,
                dma, dma((8,)), dma, dma, dma, dma, dma, dma,
                pltpu.SemaphoreType.REGULAR((rounds, 2)),
            ],
            compiler_params=pltpu.CompilerParams(
                collective_id=0, has_side_effects=True, vmem_limit_bytes=48 * 1024 * 1024
            ),
        )(*(pltpu.with_memory_space_constraint(operand, pltpu.HBM) for operand in (tensor, density, band_mask)))

    placed = (P("ri", "row", "col"), P("col", None, None), P("col", None))
    return jax.shard_map(
        per_device, mesh=mesh, in_specs=placed, out_specs=P("col", "row"), check_vma=False
    )
```

```python
import jax
import jax.numpy as jnp
from jax import lax
from jax.experimental import pallas as pl
from jax.experimental.pallas import tpu as pltpu
from jax.sharding import PartitionSpec as P

CORES = 2
BF16 = jnp.bfloat16
F32 = jnp.float32
MESH = pl.DeviceIdType.MESH


def remote(source, target, send_sem, recv_sem, device):
    return pltpu.make_async_remote_copy(
        src_ref=source, dst_ref=target, send_sem=send_sem, recv_sem=recv_sem,
        device_id=device, device_id_type=MESH,
    )


def make_kernel(nx, ny, nz, col_orb, blocks, band):
    centre = band // 2
    rim = centre * col_orb
    length = blocks * col_orb
    half = ny // CORES
    order = [0]
    for step in range(1, half):
        order += [step, ny - step]
    order.append(half)
    phases = [[0]] + [[2 * p - 1, 2 * p] for p in range(1, half)] + [[ny - 1]]

    def column_slot(offset):
        return (0, offset) if offset < half else (1, ny - 1 - offset)

    slot_at = {column_slot(offset): at for at, offset in enumerate(order)}

    def reach(p):
        rows = ny if p >= half else max(1 + 2 * p, 0)
        return rows, (min(max(p + 1, 0), half), max(p, 0))

    early = reach(half - 2)[0]

    def parts(side):
        found = []
        rows, slots = 0, 0
        for p in (half - 3, half - 2, half - 1, half):
            now, upto = reach(p)
            upto = upto[side]
            found.append(((max(rows, early), max(now, early)), (0, 0), (rows, now, 0, slots)))
            found.append(((0, 0), (slots, upto), (0, now, slots, upto)))
            rows, slots = now, upto
        return found

    def used(region):
        return region[1] > region[0] and region[3] > region[2]

    rounds = []
    while 2 ** len(rounds) < nz // 2:
        rounds.append(2 ** len(rounds))

    def kernel(
        tensor, density, band_mask, out,
        mask, ext, dens, dens_low, dens_high, big, mixed,
        x_own, x_send, x_recv, z_send, z_recv, y_send, y_recv, gathered,
        mask_sem, own_sem, a_send, a_recv, c_send, c_recv, h_send, h_recv, d_sem, d_send, d_recv,
        xs_sem, xr_sem, zs_sem, zr_sem, ys_sem, yr_sem, bs_sem, br_sem, far,
    ):
        state = []

        def phase(name):
            pass

        ri = lax.axis_index("ri")
        y = lax.axis_index("row")
        z = lax.axis_index("col")
        x = ri // CORES
        core = lax.rem(ri, CORES)
        per_block = tensor.shape[1]

        def place(to_x=x, to_core=core, to_y=y, to_z=z):
            return {"ri": to_x * CORES + to_core, "row": to_y, "col": to_z}

        z_up = lax.rem(z + 1, nz)
        z_down = lax.rem(z + nz - 1, nz)

        phase("p0_prep")
        barrier = pltpu.get_barrier_semaphore()
        partners = [place(to_y=lax.rem(y + k, ny)) for k in range(1, ny)]
        partners += [place(to_core=1 - core)]
        for k in range(1, nx):
            partners += [place(lax.rem(x + k, nx), flip) for flip in (core, 1 - core)]
        partners += [place(to_core=flip, to_z=to) for flip in (core, 1 - core) for to in (z_up, z_down)]
        for partner in partners:
            pl.semaphore_signal(barrier, inc=1, device_id=partner, device_id_type=MESH)

        load = pltpu.make_async_copy(density, dens, d_sem)
        load.start()
        masks = pltpu.make_async_copy(band_mask, mask, mask_sem)
        masks.start()
        middle = pl.ds(rim, length)
        own = pltpu.make_async_copy(tensor.at[y], ext.at[core, 0, :, :, :, middle], own_sem)
        own.start()
        big[...] = jnp.zeros_like(big)
        phase("p1_barrier")
        pl.semaphore_wait(barrier, len(partners))
        phase("p2_start")

        def far_signal(r):
            for side, to in ((0, lax.rem(z + nz - rounds[r], nz)), (1, lax.rem(z + rounds[r], nz))):
                pl.semaphore_signal(far.at[r, side], inc=1, device_id=place(to_z=to), device_id_type=MESH)

        def far_wait(r):
            for side in range(2):
                pl.semaphore_wait(far.at[r, side], 1)

        started = [None]
        for at in range(1, ny):
            to = lax.rem(y + ny - order[at], ny)
            started.append(remote(tensor.at[to], ext.at[core, at, :, :, :, middle], a_send, a_recv.at[at - 1], place(to_y=to)))

        def begin(p):
            if 0 < p <= half:
                for at in phases[p]:
                    started[at].start()

        begin(1)
        begin(2)
        load.wait()
        masks.wait()
        for b in range(blocks):
            for c in range(band):
                weight = mask[b, c].astype(F32)
                rows = slice(b * col_orb, (b + 1) * col_orb)
                dens[c, rows, :] = (dens[c, rows, :].astype(F32) * weight).astype(BF16)
        d_up = remote(dens.at[pl.ds(centre + 1, centre), pl.ds(length - rim, rim)], dens_low, d_send, d_recv, place(to_z=z_up))
        d_down = remote(dens.at[pl.ds(0, centre), pl.ds(0, rim)], dens_high, d_send, d_recv, place(to_z=z_down))
        d_up.start()
        d_down.start()
        if rounds:
            far_signal(0)

        def tile(e, t):
            row, col = e - 2 * (t // 2), t % 2
            return slice(row * col_orb, (row + 1) * col_orb), slice(col * col_orb, (col + 1) * col_orb)

        for t in range(blocks):
            for e in range(max(t, centre), min(t + band, centre + blocks)):
                rows, cols = tile(e, t)
                local = e - centre
                big[t // 2, rows, cols] = dens[band - 1 - (e - t), local * col_orb : (local + 1) * col_orb, :]

        def halo_copies(at, source):
            side, slot = column_slot(order[at])
            left = remote(ext.at[source, at, :, :, :, pl.ds(rim, rim)], ext.at[source, at, :, :, :, pl.ds(rim + length, rim)],
                          h_send, h_recv.at[slot], place(to_core=side, to_z=z_down))
            right = remote(ext.at[source, at, :, :, :, pl.ds(length, rim)], ext.at[source, at, :, :, :, pl.ds(0, rim)],
                           h_send, h_recv.at[slot], place(to_core=side, to_z=z_up))
            return left, right

        def over_copy(at, source):
            whole = ext.at[source, at, :, :, :, middle]
            return remote(whole, whole, c_send, c_recv.at[at], place(to_core=1 - core))

        def forward(p):
            for at in phases[p]:
                phase(f"p3_arrive{at}")
                if at == 0:
                    own.wait()
                else:
                    started[at].wait_recv()
                for copy in (*halo_copies(at, core), over_copy(at, core)):
                    copy.start()

        def density_rims():
            both = dens.at[pl.ds(0, centre), pl.ds(0, 2 * rim)]
            remote(both, both, d_send, d_recv, place()).wait()
            for t in range(blocks):
                for e in range(t, t + band):
                    rows, cols = tile(e, t)
                    c = band - 1 - (e - t)
                    if e < centre:
                        big[t // 2, rows, cols] = dens_low[c - centre - 1, e * col_orb : (e + 1) * col_orb, :]
                    elif e >= centre + blocks:
                        to = e - centre - blocks
                        big[t // 2, rows, cols] = dens_high[c, to * col_orb : (to + 1) * col_orb, :]

        depth = big.shape[1]
        width = big.shape[2]

        def mix(side, slot):
            at = slot_at[side, slot]
            for source in range(CORES):
                for u in range(big.shape[0]):
                    rows = ext[source, at, :, :, :, u * width : u * width + depth].reshape(-1, depth)
                    value = jnp.dot(rows, big[u], preferred_element_type=F32)
                    at_row = source * length + u * width
                    mixed[at_row : at_row + width, slot * 128 : (slot + 1) * 128] = value.T.astype(BF16)

        def terms(region):
            n0, n1, m0, m1 = region
            total = None
            for source in range(CORES):
                rows = ext[source, n0:n1, :, :, :, rim : rim + length].reshape(-1, length)
                value = jnp.dot(rows, mixed[source * length : (source + 1) * length, m0 * 128 : m1 * 128], preferred_element_type=F32)
                total = value if total is None else total + value
            total = total.reshape(n1 - n0, per_block, nx, -1, (m1 - m0) * 128)
            kept = None
            for to in range(nx):
                value = total[:, :, to]
                x_send[to, n0:n1, :, :, m0 * 128 : m1 * 128] = value.astype(BF16)
                kept = value if kept is None else jnp.where(x == to, value, kept)
            x_own[n0:n1, :, :, m0 * 128 : m1 * 128] = kept

        def x_copy(k, part, region):
            n0, n1, m0, m1 = region
            at = (pl.ds(n0, n1 - n0), slice(None), slice(None), pl.ds(m0 * 128, (m1 - m0) * 128))
            to = lax.rem(x + k, nx)
            return remote(x_send.at[(to, *at)], x_recv.at[(k - 1, *at)], xs_sem, xr_sem.at[part],
                          place(to_x=to))

        def advance(*chosen):
            for side in range(CORES):
                @pl.when(core == side)
                def _(side=side):
                    for part in chosen:
                        arrived, mixing, region = parts(side)[part]
                        for slot in range(*mixing):
                            rims = ext.at[:, slot_at[side, slot], :, :, :, pl.ds(0, 2 * rim)]
                            remote(rims, rims, h_send, h_recv.at[slot], place()).wait_recv()
                        for at in range(*arrived):
                            over_copy(at, 1 - side).wait_recv()
                        for slot in range(*mixing):
                            mix(side, slot)
                        if not used(region):
                            continue
                        terms(region)
                        for k in range(1, nx):
                            x_copy(k, part, region).start()

        def z_copy(part, region, at, b):
            lanes = pl.ds(region[2] * 128, (region[3] - region[2]) * 128)
            to = lax.rem(y + order[at], ny) * per_block + b
            k = lax.rem(to + nz - z, nz)
            slot = lax.rem(k + nz - 1, nz)
            return k, remote(z_send.at[to, :, lanes], z_recv.at[slot, :, lanes], zs_sem, zr_sem,
                             place(to_z=to))

        def settle(*chosen):
            for side in range(CORES):
                @pl.when(core == side)
                def _(side=side):
                    for part in chosen:
                        region = parts(side)[part][2]
                        if not used(region):
                            continue
                        n0, n1, m0, m1 = region
                        lanes = pl.ds(m0 * 128, (m1 - m0) * 128)
                        landed = x_recv.at[:, pl.ds(n0, n1 - n0), :, :, lanes]
                        remote(landed, landed, xs_sem, xr_sem.at[part], place()).wait_recv()
                        for at in range(n0, n1):
                            total = x_own[at, :, :, lanes]
                            for k in range(1, nx):
                                total += x_recv[k - 1, at, :, :, lanes].astype(F32)
                            block = lax.rem(y + order[at], ny)
                            x_own[at, :, :, lanes] = total
                            z_send[pl.ds(block * per_block, per_block), :, lanes] = total.astype(BF16)

                            @pl.when(block == z // per_block)
                            def _(at=at, lanes=lanes):
                                y_send[:, lanes] = x_own[at, lax.rem(z, per_block), :, lanes]
                        for near in (False, True):
                            for at in range(n0, n1):
                                for b in range(per_block):
                                    k, copy = z_copy(part, region, at, b)
                                    close = (k <= nz // 4) | (k >= nz - nz // 4)
                                    wanted = (k != 0) & close if near else jnp.logical_not(close)

                                    @pl.when(wanted)
                                    def _(copy=copy):
                                        copy.start()

        sent, waited = 1, 0
        for p in range(max(half - 1, 0)):
            forward(p)
            if p == half - 2:
                density_rims()
                phase("p4_a0")
                advance(0, 1)
                phase("p4_over")
            for at in phases[p]:
                over_copy(at, 1 - core).wait_recv()
            if 0 < p < half - 2:
                begin(p + 2)
            if 1 <= p < len(rounds):
                far_wait(p - 1)
                far_signal(p)
                sent, waited = p + 1, p
        if half == 1:
            density_rims()
        phase("p4_a1")
        advance(2, 3)
        forward(half - 1)
        if half > 2:
            begin(half)
        phase("p4_b1")
        advance(4)
        for r in range(waited, len(rounds)):
            if r >= sent:
                far_signal(r)
            far_wait(r)
        phase("p5_za")
        settle(0, 1, 2, 3)
        phase("p4_b2")
        advance(5)
        forward(half)
        phase("p4_c1")
        advance(6)
        phase("p4_c2")
        advance(7)
        phase("p5_zb")
        settle(4, 5)
        phase("p5_zc")
        settle(6, 7)
        phase("p7_zwait")
        landed = z_recv.at[pl.ds(0, nz - 1)]
        remote(landed, landed, zs_sem, zr_sem, place()).wait_recv()
        total = y_send[...]
        for slot in range(nz - 1):
            total += z_recv[slot].astype(F32)
        for slot in range(half):
            y_recv[half + slot] = total[:, slot * 128 : (slot + 1) * 128]
        phase("p8_ywait")

        def y_copy(slot):
            to = lax.rem(y + core * (ny - 1) + slot * (1 - 2 * core), ny)
            return remote(y_recv.at[half + slot], y_recv.at[slot], ys_sem, yr_sem, place(to_y=to))

        def y_all(side):
            whole = y_recv.at[pl.ds(0, half - 1 + side)]
            return remote(whole, whole, ys_sem, yr_sem, place())

        for slot in range(1, half):
            y_copy(slot).start()
        for side in range(CORES):
            @pl.when(core == side)
            def _(side=side):
                if side == 1:
                    y_copy(0).start()
                if half - 1 + side > 0:
                    y_all(side).wait_recv()
                if side == 0:
                    y_recv[0] = y_recv[half]

        total = y_recv[0]
        for slot in range(1, half):
            total += y_recv[slot]
        gathered[ri] = total
        phase("p9_bwait")

        def b_copy(k, source):
            device = {"ri": lax.rem(ri + k, CORES * nx), "row": y, "col": z}
            return remote(gathered.at[source], gathered.at[source], bs_sem, br_sem, device)

        for k in range(1, CORES * nx):
            b_copy(k, ri).start()
        spread = gathered.at[pl.ds(0, CORES * nx - 1)]
        remote(spread, spread, bs_sem, br_sem, place()).wait_recv()
        run = gathered.shape[1]
        for k in range(nx):
            out[k * run : (k + 1) * run, :] = gathered[CORES * k] + gathered[CORES * k + 1]
        phase("pa_end")

        for view, sem in (
            (ext.at[core, pl.ds(1, ny - 1), :, :, :, middle], a_send),
            (ext.at[core, :, :, :, :, middle], c_send),
            (ext.at[core, :, :, :, :, pl.ds(0, 2 * rim)], h_send),
            (x_send.at[pl.ds(0, nx - 1)], xs_sem),
            (z_send.at[pl.ds(0, nz - 1)], zs_sem),
            (spread, bs_sem),
        ):
            remote(view, view, sem, sem, place()).wait_send()
        for side in range(CORES):
            @pl.when(core == side)
            def _(side=side):
                if half - 1 + side > 0:
                    y_all(side).wait_send()
        phase(None)

    return kernel, max(len(rounds), 1)


def solution(mesh):
    nx = mesh.shape["ri"] // CORES
    ny = mesh.shape["row"]
    nz = mesh.shape["col"]

    def per_device(three_centre, density_band, band_mask):
        funcs, block_rows, length = three_centre.shape
        blocks, band = band_mask.shape
        col_orb = density_band.shape[2]
        rows = block_rows * ny
        run = rows // (nz * nx)
        per_block = nz // ny
        centre = band // 2
        rim = centre * col_orb
        half = ny // CORES
        m_rows = half * block_rows
        tensor = three_centre.reshape(funcs, per_block, nx, run, length)
        density = jnp.transpose(density_band, (1, 0, 2))
        dma = pltpu.SemaphoreType.DMA
        kernel, rounds = make_kernel(nx, ny, nz, col_orb, blocks, band)
        return pl.pallas_call(
            kernel,
            out_shape=jax.ShapeDtypeStruct((rows // nz, block_rows), F32),
            in_specs=[
                pl.BlockSpec(memory_space=pltpu.HBM),
                pl.BlockSpec(memory_space=pltpu.HBM),
                pl.BlockSpec(memory_space=pltpu.HBM),
            ],
            out_specs=pl.BlockSpec(memory_space=pltpu.VMEM),
            scratch_shapes=[
                pltpu.SMEM((blocks, band), jnp.int32),
                pltpu.VMEM((CORES, ny, per_block, nx, run, length + 2 * rim), BF16),
                pltpu.VMEM(density.shape, BF16),
                pltpu.VMEM((centre, rim, col_orb), BF16),
                pltpu.VMEM((centre, rim, col_orb), BF16),
                pltpu.VMEM((blocks // 2, (band + 1) * col_orb, 2 * col_orb), BF16),
                pltpu.VMEM((CORES * length, m_rows), BF16),
                pltpu.VMEM((ny, per_block, run, m_rows), F32),
                pltpu.VMEM((nx, ny, per_block, run, m_rows), BF16),
                pltpu.VMEM((nx - 1, ny, per_block, run, m_rows), BF16),
                pltpu.VMEM((nz, run, m_rows), BF16),
                pltpu.VMEM((nz, run, m_rows), BF16),
                pltpu.VMEM((run, m_rows), F32),
                pltpu.VMEM((2 * half, run, block_rows), F32),
                pltpu.VMEM((CORES * nx, run, block_rows), F32),
                dma, dma, dma, dma((ny - 1,)), dma, dma((ny,)), dma, dma((half,)), dma, dma, dma,
                dma, dma((8,)), dma, dma, dma, dma, dma, dma,
                pltpu.SemaphoreType.REGULAR((rounds, 2)),
            ],
            compiler_params=pltpu.CompilerParams(
                collective_id=0, has_side_effects=True, vmem_limit_bytes=48 * 1024 * 1024
            ),
        )(*(pltpu.with_memory_space_constraint(operand, pltpu.HBM) for operand in (tensor, density, band_mask)))

    placed = (P("ri", "row", "col"), P("col", None, None), P("col", None))
    return jax.shard_map(
        per_device, mesh=mesh, in_specs=placed, out_specs=P("col", "row"), check_vma=False
    )
```
